32 devices in a mesh: groups: 2 (over x), docs: 16 (over z, y, core).
Axes of the slice: x: 2, y: 2, z: 4, core: 2. Of those that a mesh axis runs over, the one named last changes fastest.
Arguments:
- embeddings: bfloat16 [4096, 1024], P(('groups', 'docs')), parts along dimension 0, may hold values from -100 to 100
- labels: int32 [4096], P(('groups', 'docs')), parts along dimension 0, may hold values from 0 to 15, as said below
- row_slot: int32 [4096], P(('groups', 'docs')), parts along dimension 0, may hold values from 0 to 2047, as said below
Outputs:
- density: float32 [4096], P(('groups', 'docs')), parts along dimension 0
- neighbour_mean: bfloat16 [4096, 1024], P(('groups', 'docs')), parts along dimension 0
The draws below stay inside these ranges and needn't reach their ends.
There are 2 independent parts, one for each index of `groups`. The reference program is written for one: setup_inputs(seed, part) draws one part's arguments, and reference() takes and returns one part's arrays. A program takes and returns all parts, laid end to end along the dimension named above; each array names one. Nothing has to cross between parts.
Inputs may be any that keep to these rules, and one draw needn't show every extreme that they name: row_slot is a permutation of 0 to 2047; at most 16 documents of one device take rows of one block, and some device places exactly 16 documents in some block. All documents in one block share one label; documents with equal labels lie in blocks at most 3 apart, and some label spans 4 blocks.
All inputs are finite; a program needn't handle non-finite values.
Results may differ from the reference program's by a relative error of at most 0.0029.
Values may be sent and summed in bfloat16 or wider, within the bound.
A program may use at most 64 MiB of HBM per device.

```python
import math
import jax
import jax.numpy as jnp
from jax import lax

D = 1024
ROWS_DEV = 128
REACH = 3
CAP = 16
TOKENS = 2048
N_DOCS = 16


def layout(base_key):
    device_total = N_DOCS
    block_rows = ROWS_DEV
    streams = jax.random.split(jax.random.fold_in(base_key, 7), 7)
    offsets = jnp.arange(device_total * CAP, dtype=jnp.int32) // CAP
    favored = jax.random.randint(streams[0], (), 0, device_total)
    tickets = jax.random.permutation(streams[1], device_total * CAP).astype(jnp.int32)
    tickets = jnp.where(offsets == favored, tickets - device_total * CAP, tickets)
    ordering = jnp.argsort(tickets)
    chosen = offsets[ordering[:block_rows]]
    per_offset = jnp.sum((chosen[:, None] == jnp.arange(device_total, dtype=jnp.int32)[None, :]).astype(jnp.int32), axis=0)
    relabel = jax.random.permutation(streams[2], device_total).astype(jnp.int32)
    sent = per_offset[(relabel[None, :] - relabel[:, None]) % device_total]
    run_ends = jnp.cumsum(sent, axis=1)
    positions = jnp.arange(block_rows, dtype=jnp.int32)
    target = jnp.sum((run_ends[:, None, :] <= positions[None, :, None]).astype(jnp.int32), axis=2)
    run_starts = run_ends - sent
    slot_rank = positions[None, :] - jnp.take_along_axis(run_starts, target, axis=1)
    earlier_sources = jnp.cumsum(sent, axis=0) - sent
    sorted_slots = target * block_rows + jnp.take_along_axis(earlier_sources, target, axis=1) + slot_rank
    shuffles = jax.vmap(lambda one_key: jax.random.permutation(one_key, block_rows))(jax.random.split(streams[3], device_total)).astype(jnp.int32)
    slot_of_row = jnp.take_along_axis(sorted_slots, shuffles, axis=1).reshape(-1).astype(jnp.int32)
    lengths = jax.random.randint(streams[4], (device_total,), 1, REACH + 2)
    forced = jax.random.randint(streams[5], (), 0, max(1, device_total // (REACH + 2)))
    lengths = lengths.at[forced].set(REACH + 1)
    bounds = jnp.cumsum(lengths)
    cluster = jnp.sum((bounds[None, :] <= jnp.arange(device_total, dtype=jnp.int32)[:, None]).astype(jnp.int32), axis=1)
    cluster_names = jax.random.permutation(streams[6], device_total).astype(jnp.int32)
    return (slot_of_row, cluster, cluster_names[cluster])


def draw_row_slot(key, part):
    slot_of_row, cluster, block_label = layout(key)
    return slot_of_row


def draw_labels(key, part):
    slot_of_row, cluster, block_label = layout(key)
    return block_label[slot_of_row // ROWS_DEV].astype(jnp.int32)


def draw_embeddings(key, part):
    slot_of_row, cluster, block_label = layout(key)
    streams = jax.random.split(jax.random.fold_in(key, 11), 2)
    centers = jnp.clip(jax.random.normal(streams[0], (N_DOCS, D), jnp.float32), -5.0, 5.0)
    noise = jnp.clip(jax.random.normal(streams[1], (TOKENS, D), jnp.float32), -5.0, 5.0)
    slot_cluster = cluster[jnp.arange(TOKENS, dtype=jnp.int32) // ROWS_DEV]
    by_slot = 0.5 * centers[slot_cluster] + 0.87 * noise
    return by_slot[slot_of_row].astype(jnp.bfloat16)


def setup_inputs(seed: int = 0, part: int = 0) -> dict:
    key_of = jax.random.split(jax.random.key(seed), 4)
    part_keys = jax.random.split(jax.random.fold_in(key_of[3], part), 4)
    embeddings = draw_embeddings(jax.random.fold_in(jax.random.fold_in(key_of[3], part), 71), part)
    labels = draw_labels(jax.random.fold_in(jax.random.fold_in(key_of[3], part), 71), part)
    row_slot = draw_row_slot(jax.random.fold_in(jax.random.fold_in(key_of[3], part), 71), part)
    return dict(embeddings=embeddings, labels=labels, row_slot=row_slot)


neg_large = -1e+30
kernel_gain = 4.0

def side_terms(scores, same_label, values):
    masked = jnp.where(same_label, scores, neg_large)
    row_max = lax.optimization_barrier(jnp.max(masked, axis=1))
    weights = jnp.where(same_label, jnp.exp(masked - row_max[:, None]), 0.0)
    row_total = lax.optimization_barrier(jnp.sum(weights, axis=1))
    rounded = weights.astype(jnp.bfloat16)
    row_accum = jnp.dot(rounded, values, preferred_element_type=jnp.float32)
    return (row_max, row_total, row_accum)

def block_terms(own_x, own_tag, far_x, far_tag, exclude_self):
    feature_width = own_x.shape[1]
    scores = jnp.dot(own_x, far_x.T, preferred_element_type=jnp.float32) * (kernel_gain / math.sqrt(feature_width))
    same_label = own_tag[:, None] == far_tag[None, :]
    if exclude_self:
        positions = jnp.arange(own_x.shape[0], dtype=jnp.int32)
        same_label = same_label & (positions[:, None] != positions[None, :])
    return side_terms(scores, same_label, far_x)

def combine(first_terms, second_terms):
    row_max = jnp.maximum(first_terms[0], second_terms[0])
    scale_first = jnp.exp(first_terms[0] - row_max)
    scale_second = jnp.exp(second_terms[0] - row_max)
    row_total = first_terms[1] * scale_first + second_terms[1] * scale_second
    row_accum = first_terms[2] * scale_first[:, None] + second_terms[2] * scale_second[:, None]
    return (row_max, row_total, row_accum)

def reference(embeddings, labels, row_slot):
    block_rows = ROWS_DEV
    device_total = N_DOCS
    blocks_x = jnp.zeros((TOKENS, D), jnp.bfloat16).at[row_slot].set(embeddings).reshape(device_total, block_rows, D)
    blocks_tag = jnp.zeros((TOKENS,), jnp.int32).at[row_slot].set(labels + 1).reshape(device_total, block_rows)
    nothing = (jnp.full((block_rows,), neg_large, jnp.float32), jnp.zeros((block_rows,), jnp.float32), jnp.zeros((block_rows, D), jnp.float32))

    def one_block(block_index):
        own_x = blocks_x[block_index]
        own_tag = blocks_tag[block_index]
        running = block_terms(own_x, own_tag, own_x, own_tag, True)

        def with_pairs(far_block, far_labels):
            return block_terms(own_x, own_tag, far_block, far_labels, False)

        def without_pairs(far_block, far_labels):
            return nothing
        for distance in range(1, REACH + 1):
            for direction in (1, -1):
                partner = block_index + direction * distance
                inside = (partner >= 0) & (partner < device_total)
                partner_safe = jnp.clip(partner, 0, device_total - 1).astype(jnp.int32)
                far_block = blocks_x[partner_safe]
                far_labels = jnp.where(inside, blocks_tag[partner_safe], 0)
                has_pairs = jnp.any(own_tag[:, None] == far_labels[None, :])
                partial_terms = lax.cond(has_pairs, with_pairs, without_pairs, far_block, far_labels)
                running = combine(running, partial_terms)
        row_max, row_total, row_accum = running
        return (row_max + jnp.log(row_total), (row_accum / row_total[:, None]).astype(jnp.bfloat16))
    densities, means = lax.map(one_block, jnp.arange(device_total, dtype=jnp.int32))
    return (densities.reshape(-1)[row_slot], means.reshape(TOKENS, D)[row_slot])
```

```python
import math

import jax
import jax.numpy as jnp
from jax import lax
from jax.sharding import PartitionSpec as P

neg_large = -1e30
kernel_gain = 4.0


def per_device(embeddings, labels, row_slot):
    my_index = lax.axis_index("docs")
    row_count, feature_width = embeddings.shape
    all_x = lax.all_gather(embeddings, "docs", axis=0, tiled=True)
    all_labels = lax.all_gather(labels, "docs", axis=0, tiled=True)
    scores = jnp.dot(embeddings, all_x.T, preferred_element_type=jnp.float32) * (
        kernel_gain / math.sqrt(feature_width)
    )
    mine = my_index * row_count + jnp.arange(row_count, dtype=jnp.int32)
    every = jnp.arange(all_x.shape[0], dtype=jnp.int32)
    near = (labels[:, None] == all_labels[None, :]) & (mine[:, None] != every[None, :])
    masked = jnp.where(near, scores, neg_large)
    row_max = jnp.max(masked, axis=1)
    weights = jnp.where(near, jnp.exp(masked - row_max[:, None]), 0.0)
    row_total = jnp.sum(weights, axis=1)
    accum = jnp.dot(weights.astype(jnp.bfloat16), all_x, preferred_element_type=jnp.float32)
    return row_max + jnp.log(row_total), (accum / row_total[:, None]).astype(jnp.bfloat16)


def solution(mesh):
    return jax.shard_map(
        per_device,
        mesh=mesh,
        in_specs=(P(("groups", "docs"), None), P(("groups", "docs")), P(("groups", "docs"))),
        out_specs=(P(("groups", "docs")), P(("groups", "docs"), None)),
        check_vma=False,
    )
```

```python
import functools
import math

import jax
import jax.numpy as jnp
from jax import lax
from jax.experimental import pallas as pl
from jax.experimental.pallas import tpu as pltpu
from jax.sharding import PartitionSpec as P

MESH = pl.DeviceIdType.MESH
CORES = 2
PIECES = 2

neg_large = -1e30
kernel_gain = 4.0


def chip_grid(device_count):
    chips = device_count // CORES
    fast = 1
    while (2 * fast) * (2 * fast) <= chips and chips % (2 * fast) == 0:
        fast *= 2
    return chips // fast, fast


def kernel(
    grid_slow, grid_fast, x_ref, lab_ref, dens_ref, mean_ref,
    buf, labs, acc, row_max, row_total, send_sem, recv_sem, lsend_sem, lrecv_sem, own_sem,
):
    rows, width = x_ref.shape
    part = rows // PIECES
    me = lax.axis_index("docs")
    core = lax.rem(me, CORES)
    chip = me // CORES
    y = lax.rem(chip, grid_fast)
    z = chip // grid_fast

    def device(zz, yy, cc):
        return (zz * grid_fast + yy) * CORES + cc

    targets = (
        (z > 0, device(z - 1, y, core)),
        (z < grid_slow - 1, device(z + 1, y, core)),
        (y > 0, device(z, y - 1, core)),
        (y < grid_fast - 1, device(z, y + 1, core)),
        (z >= 0, device(z, y, 1 - core)),
    )

    barrier = pltpu.get_barrier_semaphore()
    for there, target in targets:
        @pl.when(there)
        def _():
            pl.semaphore_signal(barrier, inc=1, device_id={"docs": target}, device_id_type=MESH)
    pl.semaphore_wait(barrier, sum(there.astype(jnp.int32) for there, _ in targets))

    def data_of(slot):
        return buf.at[pl.ds(pl.multiple_of(slot * part, part), part)]

    def copies(direction, zz, yy, piece, own):
        slot = device(zz, yy, core) * PIECES + piece
        sem = ((zz * grid_fast + yy) * PIECES) + piece
        target = {"docs": targets[direction][1]}
        data_src = x_ref.at[pl.ds(piece * part, part)] if own else data_of(slot)
        lab_src = lab_ref if own else labs.at[slot]
        return (
            pltpu.make_async_remote_copy(
                lab_src, labs.at[slot], lsend_sem.at[direction, sem], lrecv_sem.at[slot],
                device_id=target, device_id_type=MESH,
            ),
            pltpu.make_async_remote_copy(
                data_src, data_of(slot), send_sem.at[direction, sem], recv_sem.at[slot],
                device_id=target, device_id_type=MESH,
            ),
        )

    def each(directions, wanted, zz, yy, piece, own, act):
        for direction, want in zip(directions, wanted):
            @pl.when(jnp.logical_and(targets[direction][0], want))
            def _():
                for copy in copies(direction, zz, yy, piece, own):
                    act(copy)

    start = lambda copy: copy.start()
    finish = lambda copy: copy.wait_send()

    def arrived(zz, yy, cc, piece):
        slot = device(zz, yy, cc) * PIECES + piece
        for ref, send, recv in (
            (labs.at[slot], lsend_sem, lrecv_sem), (data_of(slot), send_sem, recv_sem)
        ):
            pltpu.make_async_remote_copy(
                ref, ref, send.at[0, 0], recv.at[slot],
                device_id={"docs": targets[4][1]}, device_id_type=MESH,
            ).wait_recv()

    yes = z >= 0
    for piece in range(PIECES):
        each((2, 3, 0, 1, 4), (yes,) * 5, z, y, piece, True, start)
    own_rows = buf.at[pl.ds(pl.multiple_of(me * rows, rows), rows)]
    own_copy = pltpu.make_async_copy(x_ref, own_rows, own_sem.at[0])
    own_copy.start()
    own_labs = labs.at[me * PIECES]
    own_lab_copy = pltpu.make_async_copy(lab_ref, own_labs, own_sem.at[1])
    own_lab_copy.start()

    row_max[...] = jnp.full_like(row_max, neg_large)
    row_total[...] = jnp.zeros_like(row_total)
    acc[...] = jnp.zeros_like(acc)
    label_column = jnp.transpose(
        jnp.broadcast_to(lab_ref[...].astype(jnp.float32), (rows, rows))
    )[:, :1]
    keys = CORES * rows
    gap = lax.broadcasted_iota(jnp.int32, (rows, keys), 1) - lax.broadcasted_iota(
        jnp.int32, (rows, keys), 0
    )
    own_copy.wait()
    own_lab_copy.wait()

    def compute(zz, yy):
        where = zz * grid_fast + yy
        values = buf[pl.ds(pl.multiple_of(where * keys, keys), keys), :]
        tags = jnp.concatenate(
            [labs[(where * CORES + cc) * PIECES] for cc in range(CORES)], axis=1
        ).astype(jnp.float32)
        scores = lax.dot_general(
            x_ref[...], values, (((1,), (1,)), ((), ())), preferred_element_type=jnp.float32
        ) * (kernel_gain / math.sqrt(width))
        self_gap = jnp.where(where == chip, core * rows, -keys)
        near = (label_column == tags) & (gap != self_gap)
        masked = jnp.where(near, scores, neg_large)
        before = row_max[...]
        peak = jnp.maximum(before, jnp.max(masked, axis=1, keepdims=True))
        weights = jnp.where(near, jnp.exp(masked - peak), 0.0)
        scale = jnp.exp(before - peak)
        row_max[...] = peak
        row_total[...] = row_total[...] * scale + jnp.sum(weights, axis=1, keepdims=True)
        acc[...] = acc[...] * scale + jnp.dot(
            weights.astype(jnp.bfloat16), values, preferred_element_type=jnp.float32
        )

    def visited(distance, side, reach, origin):
        place = origin + jnp.where(side == 0, -distance, distance)
        inside = (distance >= 0) & (distance < reach) & (place >= 0) & (place < reach)
        return place, inside & jnp.logical_or(distance > 0, side == 0)

    def other_columns(body):
        def one(i, carry):
            yy, valid = visited(i // 2 + 1, lax.rem(i, 2), grid_fast, y)
            @pl.when(valid)
            def _():
                body(yy)
            return carry
        lax.fori_loop(0, 2 * (grid_fast - 1), one, 0)

    def event(e, carry):
        distance = e // (2 * PIECES)
        piece = lax.rem(e // 2, PIECES)
        side = lax.rem(e, 2)

        zz, valid = visited(distance, side, grid_slow, z)
        @pl.when(valid & (distance > 0))
        def _():
            arrived(zz, y, core, piece)
            each((0, 1, 2, 3, 4), (side == 1, side == 0, yes, yes, yes), zz, y, piece, False, start)

        z1, valid1 = visited(distance - 1, side, grid_slow, z)
        @pl.when(valid1 & (piece == 0))
        def _():
            for p in range(PIECES):
                arrived(z1, y, 1 - core, p)
            compute(z1, y)

        z2, valid2 = visited(distance - 2, side, grid_slow, z)
        @pl.when(valid2)
        def _():
            def receive(yy):
                arrived(z2, yy, core, piece)
                each((2, 3, 4), (yy > y, yy < y, yes), z2, yy, piece, False, start)
            other_columns(receive)

        @pl.when(valid2 & (piece == PIECES - 1))
        def _():
            def meet(yy):
                for p in range(PIECES):
                    arrived(z2, yy, 1 - core, p)
                compute(z2, yy)
            other_columns(meet)
        return carry

    lax.fori_loop(0, 2 * PIECES * (grid_slow + 2), event, 0)

    total = row_total[...]
    density = row_max[...] + jnp.log(total)
    dens_ref[...] = jnp.transpose(jnp.broadcast_to(density, (rows, rows)))[:1, :]
    mean_ref[...] = (acc[...] / total).astype(mean_ref.dtype)

    for piece in range(PIECES):
        each((2, 3, 0, 1, 4), (yes,) * 5, z, y, piece, True, finish)

    def drain(e, carry):
        distance = e // (2 * PIECES)
        piece = lax.rem(e // 2, PIECES)
        side = lax.rem(e, 2)
        zz, valid = visited(distance, side, grid_slow, z)
        @pl.when(valid & (distance > 0))
        def _():
            each((0, 1, 2, 3, 4), (side == 1, side == 0, yes, yes, yes), zz, y, piece, False, finish)
        @pl.when(valid)
        def _():
            def sent(yy):
                each((2, 3, 4), (yy > y, yy < y, yes), zz, yy, piece, False, finish)
            other_columns(sent)
        return carry

    lax.fori_loop(0, 2 * PIECES * grid_slow, drain, 0)


def per_device(device_count, embeddings, labels, row_slot):
    rows, width = embeddings.shape
    grid_slow, grid_fast = chip_grid(device_count)
    chips = device_count // CORES
    vmem = pl.BlockSpec(memory_space=pltpu.VMEM)
    density, mean = pl.pallas_call(
        functools.partial(kernel, grid_slow, grid_fast),
        out_shape=(
            jax.ShapeDtypeStruct((1, rows), jnp.float32),
            jax.ShapeDtypeStruct((rows, width), jnp.bfloat16),
        ),
        in_specs=[vmem, vmem],
        out_specs=(vmem, vmem),
        scratch_shapes=[
            pltpu.VMEM((device_count * rows, width), jnp.bfloat16),
            pltpu.VMEM((device_count * PIECES, 1, rows), jnp.int32),
            pltpu.VMEM((rows, width), jnp.float32),
            pltpu.VMEM((rows, 1), jnp.float32),
            pltpu.VMEM((rows, 1), jnp.float32),
            pltpu.SemaphoreType.DMA((5, chips * PIECES)),
            pltpu.SemaphoreType.DMA((device_count * PIECES,)),
            pltpu.SemaphoreType.DMA((5, chips * PIECES)),
            pltpu.SemaphoreType.DMA((device_count * PIECES,)),
            pltpu.SemaphoreType.DMA((2,)),
        ],
        compiler_params=pltpu.CompilerParams(collective_id=0, has_side_effects=True),
    )(embeddings, labels.reshape(1, rows))
    return density.reshape(rows), mean


def solution(mesh):
    return jax.shard_map(
        functools.partial(per_device, mesh.shape["docs"]),
        mesh=mesh,
        in_specs=(P(("groups", "docs"), None), P(("groups", "docs")), P(("groups", "docs"))),
        out_specs=(P(("groups", "docs")), P(("groups", "docs"), None)),
        check_vma=False,
    )
```

```python
import functools
import math

import jax
import jax.numpy as jnp
from jax import lax
from jax.experimental import pallas as pl
from jax.experimental.pallas import tpu as pltpu
from jax.sharding import PartitionSpec as P

MESH = pl.DeviceIdType.MESH
CORES = 2
PIECES = 4
HALVES = 2

neg_large = -1e30
kernel_gain = 4.0


def chip_grid(device_count):
    chips = device_count // CORES
    fast = 1
    while (2 * fast) * (2 * fast) <= chips and chips % (2 * fast) == 0:
        fast *= 2
    return chips // fast, fast


def kernel(
    grid_slow, grid_fast, x_ref, lab_ref, dens_ref, mean_ref,
    buf, labs, mine, acc, row_max, row_total,
    send_sem, recv_sem, lsend_sem, lrecv_sem, own_sem, own_lab_sem,
):
    rows, width = x_ref.shape
    part = rows // PIECES
    group = PIECES // HALVES
    half_rows = rows // HALVES
    keys = CORES * half_rows
    detour = PIECES // 2 if grid_fast == 2 and grid_slow % 2 == 0 else 0
    me = lax.axis_index("docs")
    core = lax.rem(me, CORES)
    chip = me // CORES
    y = lax.rem(chip, grid_fast)
    z = chip // grid_fast
    pair = z + 1 - 2 * lax.rem(z, 2)

    def device(zz, yy, cc):
        return (zz * grid_fast + yy) * CORES + cc

    targets = (
        (z > 0, device(z - 1, y, core)),
        (z < grid_slow - 1, device(z + 1, y, core)),
        (y > 0, device(z, y - 1, core)),
        (y < grid_fast - 1, device(z, y + 1, core)),
        (z >= 0, device(z, y, 1 - core)),
    )

    barrier = pltpu.get_barrier_semaphore()
    for there, target in targets:
        @pl.when(there)
        def _():
            pl.semaphore_signal(barrier, inc=1, device_id={"docs": target}, device_id_type=MESH)

    def data_of(zz, yy, cc, piece):
        where = ((zz * grid_fast + yy) * HALVES + piece // group) * CORES + cc
        return buf.at[pl.ds(pl.multiple_of((where * group + lax.rem(piece, group)) * part, part), part)]

    own_copies = [pltpu.make_async_copy(x_ref, mine, own_sem.at[PIECES])]
    for piece in range(PIECES):
        own_copies.append(
            pltpu.make_async_copy(
                x_ref.at[pl.ds(piece * part, part)], data_of(z, y, core, piece), own_sem.at[piece]
            )
        )
    own_copies.append(pltpu.make_async_copy(lab_ref, labs.at[me], own_lab_sem.at[0]))
    for copy in own_copies:
        copy.start()
    pl.semaphore_wait(barrier, sum(there.astype(jnp.int32) for there, _ in targets))

    def data_copy(direction, zz, yy, piece, own):
        data = data_of(zz, yy, core, piece)
        return pltpu.make_async_remote_copy(
            x_ref.at[pl.ds(piece * part, part)] if own else data, data,
            send_sem.at[direction, (zz * grid_fast + yy) * PIECES + piece],
            recv_sem.at[device(zz, yy, core) * PIECES + piece],
            device_id={"docs": targets[direction][1]}, device_id_type=MESH,
        )

    def lab_copy(direction, zz, yy, own):
        slot = device(zz, yy, core)
        return pltpu.make_async_remote_copy(
            lab_ref if own else labs.at[slot], labs.at[slot],
            lsend_sem.at[direction, zz * grid_fast + yy], lrecv_sem.at[slot],
            device_id={"docs": targets[direction][1]}, device_id_type=MESH,
        )

    def each(directions, wanted, zz, yy, piece, own, act):
        for direction, want in zip(directions, wanted):
            @pl.when(jnp.logical_and(targets[direction][0], want))
            def _():
                @pl.when(piece == 0)
                def _():
                    act(lab_copy(direction, zz, yy, own))
                act(data_copy(direction, zz, yy, piece, own))

    start = lambda copy: copy.start()
    finish = lambda copy: copy.wait_send()

    def arrived(zz, yy, cc, piece):
        slot = device(zz, yy, cc)
        @pl.when(piece == 0)
        def _():
            pltpu.make_async_remote_copy(
                labs.at[slot], labs.at[slot], lsend_sem.at[0, 0], lrecv_sem.at[slot],
                device_id={"docs": targets[4][1]}, device_id_type=MESH,
            ).wait_recv()
        data = data_of(zz, yy, cc, piece)
        pltpu.make_async_remote_copy(
            data, data, send_sem.at[0, 0], recv_sem.at[slot * PIECES + piece],
            device_id={"docs": targets[4][1]}, device_id_type=MESH,
        ).wait_recv()

    yes = z >= 0
    for piece in range(PIECES):
        each((2, 3, 0, 1, 4), (yes,) * 5, z, y, piece, True, start)

    row_max[...] = jnp.full_like(row_max, neg_large)
    row_total[...] = jnp.zeros_like(row_total)
    acc[...] = jnp.zeros_like(acc)
    own_copies[-1].wait()
    label_column = jnp.transpose(
        jnp.broadcast_to(labs[me].astype(jnp.float32), (rows, rows))
    )[:, :1]
    column = lax.broadcasted_iota(jnp.int32, (rows, keys), 1)
    gap = (
        column + (column // half_rows) * (rows - half_rows)
        - lax.broadcasted_iota(jnp.int32, (rows, keys), 0)
    )
    for copy in own_copies[:-1]:
        copy.wait()

    def compute(zz, yy, half):
        where = zz * grid_fast + yy
        values = buf[pl.ds(pl.multiple_of((where * HALVES + half) * keys, keys), keys), :]
        tags = []
        for cc in range(CORES):
            tag = labs[where * CORES + cc].astype(jnp.float32)
            pieces = [tag[:, h * half_rows:(h + 1) * half_rows] for h in range(HALVES)]
            picked = pieces[0]
            for h in range(1, HALVES):
                picked = jnp.where(half == h, pieces[h], picked)
            tags.append(picked)
        tags = jnp.concatenate(tags, axis=1)
        scores = lax.dot_general(
            mine[...], values, (((1,), (1,)), ((), ())), preferred_element_type=jnp.float32
        ) * (kernel_gain / math.sqrt(width))
        self_gap = jnp.where(where == chip, core * rows - half * half_rows, CORES * rows)
        near = (label_column == tags) & (gap != self_gap)
        masked = jnp.where(near, scores, neg_large)
        before = row_max[...]
        peak = jnp.maximum(before, jnp.max(masked, axis=1, keepdims=True))
        weights = jnp.where(near, jnp.exp(masked - peak), 0.0)
        scale = jnp.exp(before - peak)
        row_max[...] = peak
        row_total[...] = row_total[...] * scale + jnp.sum(weights, axis=1, keepdims=True)
        acc[...] = acc[...] * scale + jnp.dot(
            weights.astype(jnp.bfloat16), values, preferred_element_type=jnp.float32
        )

    def meet(zz, yy, half):
        def one(p, carry):
            arrived(zz, yy, 1 - core, half * group + p)
            return carry
        lax.fori_loop(0, group, one, 0)
        compute(zz, yy, half)

    def visited(distance, side, reach, origin):
        place = origin + jnp.where(side == 0, -distance, distance)
        inside = (distance >= 0) & (distance < reach) & (place >= 0) & (place < reach)
        return place, inside & jnp.logical_or(distance > 0, side == 0)

    def other_columns(body):
        if grid_fast == 2:
            body(1 - y)
            return
        def one(i, carry):
            yy, valid = visited(i // 2 + 1, lax.rem(i, 2), grid_fast, y)
            @pl.when(valid)
            def _():
                body(yy)
            return carry
        lax.fori_loop(0, 2 * (grid_fast - 1), one, 0)

    def detoured(zz, piece):
        return (zz == pair) & (piece >= PIECES - detour)

    def along(zz, piece, side, act):
        straight = jnp.logical_not(detoured(zz, piece))
        each((0, 1, 2, 3, 4), (side == 1, side == 0, straight, straight, yes), zz, y, piece, False, act)

    def across(zz, yy, piece, act):
        each((2, 3, 4), (yy > y, yy < y, yes), zz, yy, piece, False, act)

    def to_pair(act):
        for piece in range(PIECES - detour, PIECES):
            each((0, 1), (pair < z, pair > z), z, 1 - y, piece, False, act)

    def receive(zz, yy, piece):
        arrived(zz, yy, core, piece)
        across(zz, yy, piece, start)

    def event(e, carry):
        distance = e // (2 * PIECES)
        piece = lax.rem(e // 2, PIECES)
        side = lax.rem(e, 2)
        half = piece // group

        if detour:
            @pl.when(e == 2 * PIECES * max(3, grid_slow - 1))
            def _():
                to_pair(start)

        zz, valid = visited(distance, side, grid_slow, z)
        @pl.when(valid & (distance > 0))
        def _():
            arrived(zz, y, core, piece)
            along(zz, piece, side, start)

        z1, valid1 = visited(distance - 1, side, grid_slow, z)
        z2, valid2 = visited(distance - 2, side, grid_slow, z)
        valid2 = valid2 & jnp.logical_not(detoured(z2, piece))
        @pl.when(valid2)
        def _():
            other_columns(lambda yy: receive(z2, yy, piece))

        near = valid1 & (lax.rem(piece, group) == 0)
        if grid_fast == 2:
            far = valid2 & (lax.rem(piece, group) == group - 1)
            @pl.when(near | far)
            def _():
                def one(i, carry):
                    @pl.when(jnp.where(i == 0, near, far))
                    def _():
                        meet(jnp.where(i == 0, z1, z2), jnp.where(i == 0, y, 1 - y), half)
                    return carry
                lax.fori_loop(0, 2, one, 0)
        else:
            @pl.when(near)
            def _():
                meet(z1, y, half)
            @pl.when(valid2 & (lax.rem(piece, group) == group - 1))
            def _():
                other_columns(lambda yy: meet(z2, yy, half))
        return carry

    lax.fori_loop(0, 2 * PIECES * max(4, grid_slow + 2), event, 0)
    if detour:
        for piece in range(PIECES - detour, PIECES):
            receive(pair, 1 - y, piece)
        for half in range((PIECES - detour) // group, HALVES):
            meet(pair, 1 - y, half)

    total = row_total[...]
    density = row_max[...] + jnp.log(total)
    dens_ref[...] = jnp.transpose(jnp.broadcast_to(density, (rows, rows)))[:1, :]
    mean_ref[...] = (acc[...] / total).astype(mean_ref.dtype)

    for piece in range(PIECES):
        each((2, 3, 0, 1, 4), (yes,) * 5, z, y, piece, True, finish)
    if detour:
        to_pair(finish)

    def drain(e, carry):
        distance = e // (2 * PIECES)
        piece = lax.rem(e // 2, PIECES)
        side = lax.rem(e, 2)
        zz, valid = visited(distance, side, grid_slow, z)
        @pl.when(valid & (distance > 0))
        def _():
            along(zz, piece, side, finish)
        @pl.when(valid)
        def _():
            other_columns(lambda yy: across(zz, yy, piece, finish))
        return carry

    lax.fori_loop(0, 2 * PIECES * grid_slow, drain, 0)


def per_device(device_count, embeddings, labels, row_slot):
    rows, width = embeddings.shape
    grid_slow, grid_fast = chip_grid(device_count)
    chips = device_count // CORES
    vmem = pl.BlockSpec(memory_space=pltpu.VMEM)
    density, mean = pl.pallas_call(
        functools.partial(kernel, grid_slow, grid_fast),
        out_shape=(
            jax.ShapeDtypeStruct((1, rows), jnp.float32),
            jax.ShapeDtypeStruct((rows, width), jnp.bfloat16),
        ),
        in_specs=[pl.BlockSpec(memory_space=pl.ANY), pl.BlockSpec(memory_space=pl.ANY)],
        out_specs=(vmem, vmem),
        scratch_shapes=[
            pltpu.VMEM((device_count * rows, width), jnp.bfloat16),
            pltpu.VMEM((device_count, 1, rows), jnp.int32),
            pltpu.VMEM((rows, width), jnp.bfloat16),
            pltpu.VMEM((rows, width), jnp.float32),
            pltpu.VMEM((rows, 1), jnp.float32),
            pltpu.VMEM((rows, 1), jnp.float32),
            pltpu.SemaphoreType.DMA((5, chips * PIECES)),
            pltpu.SemaphoreType.DMA((device_count * PIECES,)),
            pltpu.SemaphoreType.DMA((5, chips)),
            pltpu.SemaphoreType.DMA((device_count,)),
            pltpu.SemaphoreType.DMA((PIECES + 1,)),
            pltpu.SemaphoreType.DMA((1,)),
        ],
        compiler_params=pltpu.CompilerParams(collective_id=0, has_side_effects=True),
    )(embeddings, labels.reshape(1, rows))
    return density.reshape(rows), mean


def solution(mesh):
    return jax.shard_map(
        functools.partial(per_device, mesh.shape["docs"]),
        mesh=mesh,
        in_specs=(P(("groups", "docs"), None), P(("groups", "docs")), P(("groups", "docs"))),
        out_specs=(P(("groups", "docs")), P(("groups", "docs"), None)),
        check_vma=False,
    )
```

```python
import functools
import math

import jax
import jax.numpy as jnp
from jax import lax
from jax.experimental import pallas as pl
from jax.experimental.pallas import tpu as pltpu
from jax.sharding import PartitionSpec as P

MESH = pl.DeviceIdType.MESH
CORES = 2
PIECES = 2
HALVES = 1

neg_large = -1e30
kernel_gain = 4.0


def chip_grid(device_count):
    chips = device_count // CORES
    fast = 1
    while (2 * fast) * (2 * fast) <= chips and chips % (2 * fast) == 0:
        fast *= 2
    return chips // fast, fast


def kernel(
    grid_slow, grid_fast, x_ref, lab_ref, dens_ref, mean_ref,
    buf, labs, mine, acc, row_max, row_total,
    send_sem, recv_sem, lsend_sem, lrecv_sem, own_sem, own_lab_sem,
):
    rows, width = x_ref.shape
    part = rows // PIECES
    group = PIECES // HALVES
    half_rows = rows // HALVES
    keys = CORES * half_rows
    detour = 0
    me = lax.axis_index("docs")
    core = lax.rem(me, CORES)
    chip = me // CORES
    y = lax.rem(chip, grid_fast)
    z = chip // grid_fast
    pair = z + 1 - 2 * lax.rem(z, 2)

    def device(zz, yy, cc):
        return (zz * grid_fast + yy) * CORES + cc

    targets = (
        (z > 0, device(z - 1, y, core)),
        (z < grid_slow - 1, device(z + 1, y, core)),
        (y > 0, device(z, y - 1, core)),
        (y < grid_fast - 1, device(z, y + 1, core)),
        (z >= 0, device(z, y, 1 - core)),
    )

    barrier = pltpu.get_barrier_semaphore()
    for there, target in targets:
        @pl.when(there)
        def _():
            pl.semaphore_signal(barrier, inc=1, device_id={"docs": target}, device_id_type=MESH)

    def data_of(zz, yy, cc, piece):
        where = ((zz * grid_fast + yy) * HALVES + piece // group) * CORES + cc
        return buf.at[pl.ds(pl.multiple_of((where * group + lax.rem(piece, group)) * part, part), part)]

    own_copies = [pltpu.make_async_copy(x_ref, mine, own_sem.at[PIECES])]
    for piece in range(PIECES):
        own_copies.append(
            pltpu.make_async_copy(
                x_ref.at[pl.ds(piece * part, part)], data_of(z, y, core, piece), own_sem.at[piece]
            )
        )
    own_copies.append(pltpu.make_async_copy(lab_ref, labs.at[me], own_lab_sem.at[0]))
    for copy in own_copies:
        copy.start()
    pl.semaphore_wait(barrier, sum(there.astype(jnp.int32) for there, _ in targets))

    def data_copy(direction, zz, yy, piece, own):
        data = data_of(zz, yy, core, piece)
        return pltpu.make_async_remote_copy(
            x_ref.at[pl.ds(piece * part, part)] if own else data, data,
            send_sem.at[direction, (zz * grid_fast + yy) * PIECES + piece],
            recv_sem.at[device(zz, yy, core) * PIECES + piece],
            device_id={"docs": targets[direction][1]}, device_id_type=MESH,
        )

    def lab_copy(direction, zz, yy, own):
        slot = device(zz, yy, core)
        return pltpu.make_async_remote_copy(
            lab_ref if own else labs.at[slot], labs.at[slot],
            lsend_sem.at[direction, zz * grid_fast + yy], lrecv_sem.at[slot],
            device_id={"docs": targets[direction][1]}, device_id_type=MESH,
        )

    def each(directions, wanted, zz, yy, piece, own, act):
        for direction, want in zip(directions, wanted):
            @pl.when(jnp.logical_and(targets[direction][0], want))
            def _():
                @pl.when(piece == 0)
                def _():
                    act(lab_copy(direction, zz, yy, own))
                act(data_copy(direction, zz, yy, piece, own))

    start = lambda copy: copy.start()
    finish = lambda copy: copy.wait_send()

    def arrived(zz, yy, cc, piece):
        slot = device(zz, yy, cc)
        @pl.when(piece == 0)
        def _():
            pltpu.make_async_remote_copy(
                labs.at[slot], labs.at[slot], lsend_sem.at[0, 0], lrecv_sem.at[slot],
                device_id={"docs": targets[4][1]}, device_id_type=MESH,
            ).wait_recv()
        data = data_of(zz, yy, cc, piece)
        pltpu.make_async_remote_copy(
            data, data, send_sem.at[0, 0], recv_sem.at[slot * PIECES + piece],
            device_id={"docs": targets[4][1]}, device_id_type=MESH,
        ).wait_recv()

    yes = z >= 0
    for piece in range(PIECES):
        each((2, 3, 0, 1, 4), (yes,) * 5, z, y, piece, True, start)

    row_max[...] = jnp.full_like(row_max, neg_large)
    row_total[...] = jnp.zeros_like(row_total)
    acc[...] = jnp.zeros_like(acc)
    own_copies[-1].wait()
    label_column = jnp.transpose(
        jnp.broadcast_to(labs[me].astype(jnp.float32), (rows, rows))
    )[:, :1]
    column = lax.broadcasted_iota(jnp.int32, (rows, keys), 1)
    gap = (
        column + (column // half_rows) * (rows - half_rows)
        - lax.broadcasted_iota(jnp.int32, (rows, keys), 0)
    )
    for copy in own_copies[:-1]:
        copy.wait()

    def compute(zz, yy, half):
        where = zz * grid_fast + yy
        values = buf[pl.ds(pl.multiple_of((where * HALVES + half) * keys, keys), keys), :]
        tags = []
        for cc in range(CORES):
            tag = labs[where * CORES + cc].astype(jnp.float32)
            pieces = [tag[:, h * half_rows:(h + 1) * half_rows] for h in range(HALVES)]
            picked = pieces[0]
            for h in range(1, HALVES):
                picked = jnp.where(half == h, pieces[h], picked)
            tags.append(picked)
        tags = jnp.concatenate(tags, axis=1)
        scores = lax.dot_general(
            mine[...], values, (((1,), (1,)), ((), ())), preferred_element_type=jnp.float32
        ) * (kernel_gain / math.sqrt(width))
        self_gap = jnp.where(where == chip, core * rows - half * half_rows, CORES * rows)
        near = (label_column == tags) & (gap != self_gap)
        masked = jnp.where(near, scores, neg_large)
        before = row_max[...]
        peak = jnp.maximum(before, jnp.max(masked, axis=1, keepdims=True))
        weights = jnp.where(near, jnp.exp(masked - peak), 0.0)
        scale = jnp.exp(before - peak)
        row_max[...] = peak
        row_total[...] = row_total[...] * scale + jnp.sum(weights, axis=1, keepdims=True)
        acc[...] = acc[...] * scale + jnp.dot(
            weights.astype(jnp.bfloat16), values, preferred_element_type=jnp.float32
        )

    def meet(zz, yy, half):
        def one(p, carry):
            arrived(zz, yy, 1 - core, half * group + p)
            return carry
        lax.fori_loop(0, group, one, 0)
        compute(zz, yy, half)

    def visited(distance, side, reach, origin):
        place = origin + jnp.where(side == 0, -distance, distance)
        inside = (distance >= 0) & (distance < reach) & (place >= 0) & (place < reach)
        return place, inside & jnp.logical_or(distance > 0, side == 0)

    def other_columns(body):
        if grid_fast == 2:
            body(1 - y)
            return
        def one(i, carry):
            yy, valid = visited(i // 2 + 1, lax.rem(i, 2), grid_fast, y)
            @pl.when(valid)
            def _():
                body(yy)
            return carry
        lax.fori_loop(0, 2 * (grid_fast - 1), one, 0)

    def detoured(zz, piece):
        return (zz == pair) & (piece >= PIECES - detour)

    def along(zz, piece, side, act):
        straight = jnp.logical_not(detoured(zz, piece))
        each((0, 1, 2, 3, 4), (side == 1, side == 0, straight, straight, yes), zz, y, piece, False, act)

    def across(zz, yy, piece, act):
        each((2, 3, 4), (yy > y, yy < y, yes), zz, yy, piece, False, act)

    def to_pair(act):
        for piece in range(PIECES - detour, PIECES):
            each((0, 1), (pair < z, pair > z), z, 1 - y, piece, False, act)

    def receive(zz, yy, piece):
        arrived(zz, yy, core, piece)
        across(zz, yy, piece, start)

    def event(e, carry):
        distance = e // (2 * PIECES)
        piece = lax.rem(e // 2, PIECES)
        side = lax.rem(e, 2)
        half = piece // group

        if detour:
            @pl.when(e == 2 * PIECES * max(3, grid_slow - 1))
            def _():
                to_pair(start)

        zz, valid = visited(distance, side, grid_slow, z)
        @pl.when(valid & (distance > 0))
        def _():
            arrived(zz, y, core, piece)
            along(zz, piece, side, start)

        z1, valid1 = visited(distance - 1, side, grid_slow, z)
        z2, valid2 = visited(distance - 2, side, grid_slow, z)
        valid2 = valid2 & jnp.logical_not(detoured(z2, piece))
        @pl.when(valid2)
        def _():
            other_columns(lambda yy: receive(z2, yy, piece))

        near = valid1 & (lax.rem(piece, group) == 0)
        if grid_fast == 2:
            far = valid2 & (lax.rem(piece, group) == group - 1)
            @pl.when(near | far)
            def _():
                def one(i, carry):
                    @pl.when(jnp.where(i == 0, near, far))
                    def _():
                        meet(jnp.where(i == 0, z1, z2), jnp.where(i == 0, y, 1 - y), half)
                    return carry
                lax.fori_loop(0, 2, one, 0)
        else:
            @pl.when(near)
            def _():
                meet(z1, y, half)
            @pl.when(valid2 & (lax.rem(piece, group) == group - 1))
            def _():
                other_columns(lambda yy: meet(z2, yy, half))
        return carry

    lax.fori_loop(0, 2 * PIECES * max(4, grid_slow + 2), event, 0)
    if detour:
        for piece in range(PIECES - detour, PIECES):
            receive(pair, 1 - y, piece)
        for half in range((PIECES - detour) // group, HALVES):
            meet(pair, 1 - y, half)

    total = row_total[...]
    density = row_max[...] + jnp.log(total)
    dens_ref[...] = jnp.transpose(jnp.broadcast_to(density, (rows, rows)))[:1, :]
    mean_ref[...] = (acc[...] / total).astype(mean_ref.dtype)

    for piece in range(PIECES):
        each((2, 3, 0, 1, 4), (yes,) * 5, z, y, piece, True, finish)
    if detour:
        to_pair(finish)

    def drain(e, carry):
        distance = e // (2 * PIECES)
        piece = lax.rem(e // 2, PIECES)
        side = lax.rem(e, 2)
        zz, valid = visited(distance, side, grid_slow, z)
        @pl.when(valid & (distance > 0))
        def _():
            along(zz, piece, side, finish)
        @pl.when(valid)
        def _():
            other_columns(lambda yy: across(zz, yy, piece, finish))
        return carry

    lax.fori_loop(0, 2 * PIECES * grid_slow, drain, 0)


def per_device(device_count, embeddings, labels, row_slot):
    rows, width = embeddings.shape
    grid_slow, grid_fast = chip_grid(device_count)
    chips = device_count // CORES
    vmem = pl.BlockSpec(memory_space=pltpu.VMEM)
    density, mean = pl.pallas_call(
        functools.partial(kernel, grid_slow, grid_fast),
        out_shape=(
            pltpu.VMEM((1, rows), jnp.float32),
            pltpu.VMEM((rows, width), jnp.bfloat16),
        ),
        in_specs=[pl.BlockSpec(memory_space=pl.ANY), pl.BlockSpec(memory_space=pl.ANY)],
        out_specs=(vmem, vmem),
        scratch_shapes=[
            pltpu.VMEM((device_count * rows, width), jnp.bfloat16),
            pltpu.VMEM((device_count, 1, rows), jnp.int32),
            pltpu.VMEM((rows, width), jnp.bfloat16),
            pltpu.VMEM((rows, width), jnp.float32),
            pltpu.VMEM((rows, 1), jnp.float32),
            pltpu.VMEM((rows, 1), jnp.float32),
            pltpu.SemaphoreType.DMA((5, chips * PIECES)),
            pltpu.SemaphoreType.DMA((device_count * PIECES,)),
            pltpu.SemaphoreType.DMA((5, chips)),
            pltpu.SemaphoreType.DMA((device_count,)),
            pltpu.SemaphoreType.DMA((PIECES + 1,)),
            pltpu.SemaphoreType.DMA((1,)),
        ],
        compiler_params=pltpu.CompilerParams(collective_id=0, has_side_effects=True),
    )(embeddings, labels.reshape(1, rows))
    return density.reshape(rows), mean


def solution(mesh):
    return jax.shard_map(
        functools.partial(per_device, mesh.shape["docs"]),
        mesh=mesh,
        in_specs=(P(("groups", "docs"), None), P(("groups", "docs")), P(("groups", "docs"))),
        out_specs=(P(("groups", "docs")), P(("groups", "docs"), None)),
        check_vma=False,
    )
```

```python
import functools
import math

import jax
import jax.numpy as jnp
from jax import lax
from jax.experimental import pallas as pl
from jax.experimental.pallas import tpu as pltpu
from jax.sharding import PartitionSpec as P

MESH = pl.DeviceIdType.MESH
CORES = 2
PIECES = 2
HALVES = 1

neg_large = -1e30
kernel_gain = 4.0


def chip_grid(device_count):
    chips = device_count // CORES
    fast = 1
    while (2 * fast) * (2 * fast) <= chips and chips % (2 * fast) == 0:
        fast *= 2
    return chips // fast, fast


def kernel(
    grid_slow, grid_fast, x_ref, lab_ref, dens_ref, mean_ref,
    buf, labs, mine, acc, row_max, row_total,
    send_sem, recv_sem, lsend_sem, lrecv_sem, own_sem, own_lab_sem,
):
    rows, width = x_ref.shape
    part = rows // PIECES
    group = PIECES // HALVES
    half_rows = rows // HALVES
    keys = CORES * half_rows
    me = lax.axis_index("docs")
    core = lax.rem(me, CORES)
    chip = me // CORES
    y = lax.rem(chip, grid_fast)
    z = chip // grid_fast

    def device(zz, yy, cc):
        return (zz * grid_fast + yy) * CORES + cc

    targets = (
        (z > 0, device(z - 1, y, core)),
        (z < grid_slow - 1, device(z + 1, y, core)),
        (y > 0, device(z, y - 1, core)),
        (y < grid_fast - 1, device(z, y + 1, core)),
        (z >= 0, device(z, y, 1 - core)),
    )

    barrier = pltpu.get_barrier_semaphore()
    for there, target in targets:
        @pl.when(there)
        def _():
            pl.semaphore_signal(barrier, inc=1, device_id={"docs": target}, device_id_type=MESH)

    def data_of(zz, yy, cc, piece):
        where = ((zz * grid_fast + yy) * HALVES + piece // group) * CORES + cc
        return buf.at[pl.ds(pl.multiple_of((where * group + lax.rem(piece, group)) * part, part), part)]

    own_copies = [pltpu.make_async_copy(x_ref, mine, own_sem.at[PIECES])]
    for piece in range(PIECES):
        own_copies.append(
            pltpu.make_async_copy(
                x_ref.at[pl.ds(piece * part, part)], data_of(z, y, core, piece), own_sem.at[piece]
            )
        )
    own_copies.append(pltpu.make_async_copy(lab_ref, labs.at[me], own_lab_sem.at[0]))
    for copy in own_copies:
        copy.start()
    pl.semaphore_wait(barrier, sum(there.astype(jnp.int32) for there, _ in targets))

    def data_copy(direction, zz, yy, piece, own):
        data = data_of(zz, yy, core, piece)
        return pltpu.make_async_remote_copy(
            x_ref.at[pl.ds(piece * part, part)] if own else data, data,
            send_sem.at[direction, (zz * grid_fast + yy) * PIECES + piece],
            recv_sem.at[device(zz, yy, core) * PIECES + piece],
            device_id={"docs": targets[direction][1]}, device_id_type=MESH,
        )

    def lab_copy(direction, zz, yy, own):
        slot = device(zz, yy, core)
        return pltpu.make_async_remote_copy(
            lab_ref if own else labs.at[slot], labs.at[slot],
            lsend_sem.at[direction, zz * grid_fast + yy], lrecv_sem.at[slot],
            device_id={"docs": targets[direction][1]}, device_id_type=MESH,
        )

    def each(directions, wanted, zz, yy, piece, own, act):
        for direction, want in zip(directions, wanted):
            @pl.when(jnp.logical_and(targets[direction][0], want))
            def _():
                @pl.when(piece == 0)
                def _():
                    act(lab_copy(direction, zz, yy, own))
                act(data_copy(direction, zz, yy, piece, own))

    start = lambda copy: copy.start()
    finish = lambda copy: copy.wait_send()

    def arrived(zz, yy, cc, piece):
        slot = device(zz, yy, cc)
        @pl.when(piece == 0)
        def _():
            pltpu.make_async_remote_copy(
                labs.at[slot], labs.at[slot], lsend_sem.at[0, 0], lrecv_sem.at[slot],
                device_id={"docs": targets[4][1]}, device_id_type=MESH,
            ).wait_recv()
        data = data_of(zz, yy, cc, piece)
        pltpu.make_async_remote_copy(
            data, data, send_sem.at[0, 0], recv_sem.at[slot * PIECES + piece],
            device_id={"docs": targets[4][1]}, device_id_type=MESH,
        ).wait_recv()

    yes = z >= 0
    for piece in range(PIECES):
        each((2, 3, 0, 1, 4), (yes,) * 5, z, y, piece, True, start)

    row_max[...] = jnp.full_like(row_max, neg_large)
    row_total[...] = jnp.zeros_like(row_total)
    acc[...] = jnp.zeros_like(acc)
    own_copies[-1].wait()
    label_column = jnp.transpose(
        jnp.broadcast_to(labs[me].astype(jnp.float32), (rows, rows))
    )[:, :1]
    column = lax.broadcasted_iota(jnp.int32, (rows, keys), 1)
    gap = (
        column + (column // half_rows) * (rows - half_rows)
        - lax.broadcasted_iota(jnp.int32, (rows, keys), 0)
    )
    for copy in own_copies[:-1]:
        copy.wait()

    def compute(zz, yy, half):
        where = zz * grid_fast + yy
        values = buf[pl.ds(pl.multiple_of((where * HALVES + half) * keys, keys), keys), :]
        tags = []
        for cc in range(CORES):
            tag = labs[where * CORES + cc].astype(jnp.float32)
            pieces = [tag[:, h * half_rows:(h + 1) * half_rows] for h in range(HALVES)]
            picked = pieces[0]
            for h in range(1, HALVES):
                picked = jnp.where(half == h, pieces[h], picked)
            tags.append(picked)
        tags = jnp.concatenate(tags, axis=1)
        scores = lax.dot_general(
            mine[...], values, (((1,), (1,)), ((), ())), preferred_element_type=jnp.float32
        ) * (kernel_gain / math.sqrt(width))
        self_gap = jnp.where(where == chip, core * rows - half * half_rows, CORES * rows)
        near = (label_column == tags) & (gap != self_gap)
        masked = jnp.where(near, scores, neg_large)
        before = row_max[...]
        peak = jnp.maximum(before, jnp.max(masked, axis=1, keepdims=True))
        weights = jnp.where(near, jnp.exp(masked - peak), 0.0)
        scale = jnp.exp(before - peak)
        row_max[...] = peak
        row_total[...] = row_total[...] * scale + jnp.sum(weights, axis=1, keepdims=True)
        acc[...] = acc[...] * scale + jnp.dot(
            weights.astype(jnp.bfloat16), values, preferred_element_type=jnp.float32
        )

    def meet(zz, yy, half):
        def one(p, carry):
            arrived(zz, yy, 1 - core, half * group + p)
            return carry
        lax.fori_loop(0, group, one, 0)
        compute(zz, yy, half)

    def visited(distance, side, reach, origin):
        place = origin + jnp.where(side == 0, -distance, distance)
        inside = (distance >= 0) & (distance < reach) & (place >= 0) & (place < reach)
        return place, inside & jnp.logical_or(distance > 0, side == 0)

    def other_columns(body):
        if grid_fast == 2:
            body(1 - y)
            return
        def one(i, carry):
            yy, valid = visited(i // 2 + 1, lax.rem(i, 2), grid_fast, y)
            @pl.when(valid)
            def _():
                body(yy)
            return carry
        lax.fori_loop(0, 2 * (grid_fast - 1), one, 0)

    def along(zz, piece, side, act):
        each((0, 1, 2, 3, 4), (side == 1, side == 0, yes, yes, yes), zz, y, piece, False, act)

    def across(zz, yy, piece, act):
        each((2, 3, 4), (yy > y, yy < y, yes), zz, yy, piece, False, act)

    def receive(zz, yy, piece):
        arrived(zz, yy, core, piece)
        across(zz, yy, piece, start)

    def event(e, carry):
        distance = e // (2 * PIECES)
        piece = lax.rem(e // 2, PIECES)
        side = lax.rem(e, 2)
        half = piece // group

        @pl.when(e == 2 * PIECES * grid_slow)
        def _():
            for p in range(PIECES):
                each((2, 3, 0, 1, 4), (yes,) * 5, z, y, p, True, finish)

        zz, valid = visited(distance, side, grid_slow, z)
        @pl.when(valid & (distance > 0))
        def _():
            arrived(zz, y, core, piece)
            along(zz, piece, side, start)

        z1, valid1 = visited(distance - 1, side, grid_slow, z)
        z2, valid2 = visited(distance - 2, side, grid_slow, z)
        @pl.when(valid2)
        def _():
            other_columns(lambda yy: receive(z2, yy, piece))
            @pl.when(distance > 2)
            def _():
                along(z2, piece, side, finish)

        z3, valid3 = visited(distance - 3, side, grid_slow, z)
        @pl.when(valid3)
        def _():
            other_columns(lambda yy: across(z3, yy, piece, finish))

        near = valid1 & (lax.rem(piece, group) == 0)
        if grid_fast == 2:
            far = valid2 & (lax.rem(piece, group) == group - 1)
            @pl.when(near | far)
            def _():
                def one(i, carry):
                    @pl.when(jnp.where(i == 0, near, far))
                    def _():
                        meet(jnp.where(i == 0, z1, z2), jnp.where(i == 0, y, 1 - y), half)
                    return carry
                lax.fori_loop(0, 2, one, 0)
        else:
            @pl.when(near)
            def _():
                meet(z1, y, half)
            @pl.when(valid2 & (lax.rem(piece, group) == group - 1))
            def _():
                other_columns(lambda yy: meet(z2, yy, half))
        return carry

    lax.fori_loop(0, 2 * PIECES * (grid_slow + 2), event, 0)

    total = row_total[...]
    density = row_max[...] + jnp.log(total)
    dens_ref[...] = jnp.transpose(jnp.broadcast_to(density, (rows, rows)))[:1, :]
    mean_ref[...] = (acc[...] / total).astype(mean_ref.dtype)

    for e in range(2 * PIECES):
        last, valid = visited(grid_slow - 1, e % 2, grid_slow, z)
        @pl.when(valid)
        def _():
            other_columns(lambda yy: across(last, yy, e // 2, finish))


def per_device(device_count, embeddings, labels, row_slot):
    rows, width = embeddings.shape
    grid_slow, grid_fast = chip_grid(device_count)
    chips = device_count // CORES
    vmem = pl.BlockSpec(memory_space=pltpu.VMEM)
    density, mean = pl.pallas_call(
        functools.partial(kernel, grid_slow, grid_fast),
        out_shape=(
            pltpu.VMEM((1, rows), jnp.float32),
            pltpu.VMEM((rows, width), jnp.bfloat16),
        ),
        in_specs=[pl.BlockSpec(memory_space=pl.ANY), pl.BlockSpec(memory_space=pl.ANY)],
        out_specs=(vmem, vmem),
        scratch_shapes=[
            pltpu.VMEM((device_count * rows, width), jnp.bfloat16),
            pltpu.VMEM((device_count, 1, rows), jnp.int32),
            pltpu.VMEM((rows, width), jnp.bfloat16),
            pltpu.VMEM((rows, width), jnp.float32),
            pltpu.VMEM((rows, 1), jnp.float32),
            pltpu.VMEM((rows, 1), jnp.float32),
            pltpu.SemaphoreType.DMA((5, chips * PIECES)),
            pltpu.SemaphoreType.DMA((device_count * PIECES,)),
            pltpu.SemaphoreType.DMA((5, chips)),
            pltpu.SemaphoreType.DMA((device_count,)),
            pltpu.SemaphoreType.DMA((PIECES + 1,)),
            pltpu.SemaphoreType.DMA((1,)),
        ],
        compiler_params=pltpu.CompilerParams(collective_id=0, has_side_effects=True),
    )(embeddings, labels.reshape(1, rows))
    return density.reshape(rows), mean


def solution(mesh):
    return jax.shard_map(
        functools.partial(per_device, mesh.shape["docs"]),
        mesh=mesh,
        in_specs=(P(("groups", "docs"), None), P(("groups", "docs")), P(("groups", "docs"))),
        out_specs=(P(("groups", "docs")), P(("groups", "docs"), None)),
        check_vma=False,
    )
```

```python
import functools
import math

import jax
import jax.numpy as jnp
from jax import lax
from jax.experimental import pallas as pl
from jax.experimental.pallas import tpu as pltpu
from jax.sharding import PartitionSpec as P

MESH = pl.DeviceIdType.MESH
CORES = 2
PIECES = 2
HALVES = 1

neg_large = -1e30
kernel_gain = 4.0


def chip_grid(device_count):
    chips = device_count // CORES
    fast = 1
    while (2 * fast) * (2 * fast) <= chips and chips % (2 * fast) == 0:
        fast *= 2
    return chips // fast, fast


def kernel(
    grid_slow, grid_fast, x_ref, lab_ref, dens_ref, mean_ref,
    buf, labs, mine, acc, row_max, row_total,
    send_sem, recv_sem, lsend_sem, lrecv_sem, own_sem, own_lab_sem,
):
    rows, width = x_ref.shape
    part = rows // PIECES
    group = PIECES // HALVES
    half_rows = rows // HALVES
    keys = CORES * half_rows
    me = lax.axis_index("docs")
    core = lax.rem(me, CORES)
    chip = me // CORES
    y = lax.rem(chip, grid_fast)
    z = chip // grid_fast

    def device(zz, yy, cc):
        return (zz * grid_fast + yy) * CORES + cc

    targets = (
        (z > 0, device(z - 1, y, core)),
        (z < grid_slow - 1, device(z + 1, y, core)),
        (y > 0, device(z, y - 1, core)),
        (y < grid_fast - 1, device(z, y + 1, core)),
        (z >= 0, device(z, y, 1 - core)),
    )

    barrier = pltpu.get_barrier_semaphore()
    for there, target in targets:
        @pl.when(there)
        def _():
            pl.semaphore_signal(barrier, inc=1, device_id={"docs": target}, device_id_type=MESH)

    def data_of(zz, yy, cc, piece):
        where = ((zz * grid_fast + yy) * HALVES + piece // group) * CORES + cc
        return buf.at[pl.ds(pl.multiple_of((where * group + lax.rem(piece, group)) * part, part), part)]

    own_copies = [pltpu.make_async_copy(x_ref, mine, own_sem.at[PIECES])]
    for piece in range(PIECES):
        own_copies.append(
            pltpu.make_async_copy(
                x_ref.at[pl.ds(piece * part, part)], data_of(z, y, core, piece), own_sem.at[piece]
            )
        )
    own_copies.append(pltpu.make_async_copy(lab_ref, labs.at[me], own_lab_sem.at[0]))
    for copy in own_copies:
        copy.start()
    pl.semaphore_wait(barrier, sum(there.astype(jnp.int32) for there, _ in targets))

    def data_copy(direction, zz, yy, piece, own):
        data = data_of(zz, yy, core, piece)
        return pltpu.make_async_remote_copy(
            x_ref.at[pl.ds(piece * part, part)] if own else data, data,
            send_sem.at[direction, (zz * grid_fast + yy) * PIECES + piece],
            recv_sem.at[device(zz, yy, core) * PIECES + piece],
            device_id={"docs": targets[direction][1]}, device_id_type=MESH,
        )

    def lab_copy(direction, zz, yy, own):
        slot = device(zz, yy, core)
        return pltpu.make_async_remote_copy(
            lab_ref if own else labs.at[slot], labs.at[slot],
            lsend_sem.at[direction, zz * grid_fast + yy], lrecv_sem.at[slot],
            device_id={"docs": targets[direction][1]}, device_id_type=MESH,
        )

    def each(directions, wanted, zz, yy, piece, own, act):
        for direction, want in zip(directions, wanted):
            @pl.when(jnp.logical_and(targets[direction][0], want))
            def _():
                @pl.when(piece == 0)
                def _():
                    act(lab_copy(direction, zz, yy, own))
                act(data_copy(direction, zz, yy, piece, own))

    start = lambda copy: copy.start()
    finish = lambda copy: copy.wait_send()

    def arrived(zz, yy, cc, piece):
        slot = device(zz, yy, cc)
        @pl.when(piece == 0)
        def _():
            pltpu.make_async_remote_copy(
                labs.at[slot], labs.at[slot], lsend_sem.at[0, 0], lrecv_sem.at[slot],
                device_id={"docs": targets[4][1]}, device_id_type=MESH,
            ).wait_recv()
        data = data_of(zz, yy, cc, piece)
        pltpu.make_async_remote_copy(
            data, data, send_sem.at[0, 0], recv_sem.at[slot * PIECES + piece],
            device_id={"docs": targets[4][1]}, device_id_type=MESH,
        ).wait_recv()

    yes = z >= 0
    for piece in range(PIECES):
        each((2, 3, 0, 1, 4), (yes,) * 5, z, y, piece, True, start)

    row_max[...] = jnp.full_like(row_max, neg_large)
    row_total[...] = jnp.zeros_like(row_total)
    acc[...] = jnp.zeros_like(acc)
    own_copies[-1].wait()
    label_column = jnp.transpose(
        jnp.broadcast_to(labs[me].astype(jnp.float32), (rows, rows))
    )[:, :1]
    column = lax.broadcasted_iota(jnp.int32, (rows, keys), 1)
    gap = (
        column + (column // half_rows) * (rows - half_rows)
        - lax.broadcasted_iota(jnp.int32, (rows, keys), 0)
    )
    for copy in own_copies[:-1]:
        copy.wait()

    def compute(zz, yy, half):
        where = zz * grid_fast + yy
        values = buf[pl.ds(pl.multiple_of((where * HALVES + half) * keys, keys), keys), :]
        tags = []
        for cc in range(CORES):
            tag = labs[where * CORES + cc].astype(jnp.float32)
            pieces = [tag[:, h * half_rows:(h + 1) * half_rows] for h in range(HALVES)]
            picked = pieces[0]
            for h in range(1, HALVES):
                picked = jnp.where(half == h, pieces[h], picked)
            tags.append(picked)
        tags = jnp.concatenate(tags, axis=1)
        scores = lax.dot_general(
            mine[...], values, (((1,), (1,)), ((), ())), preferred_element_type=jnp.float32
        ) * (kernel_gain / math.sqrt(width))
        self_gap = jnp.where(where == chip, core * rows - half * half_rows, CORES * rows)
        absorb(scores, (label_column == tags) & (gap != self_gap), values)

    def compute_core(zz, yy, cc):
        slot = device(zz, yy, cc)
        values = buf[pl.ds(pl.multiple_of(slot * rows, rows), rows), :]
        scores = lax.dot_general(
            mine[...], values, (((1,), (1,)), ((), ())), preferred_element_type=jnp.float32
        ) * (kernel_gain / math.sqrt(width))
        absorb(scores, label_column == labs[slot].astype(jnp.float32), values)

    def absorb(scores, near, values):
        masked = jnp.where(near, scores, neg_large)
        before = row_max[...]
        peak = jnp.maximum(before, jnp.max(masked, axis=1, keepdims=True))
        weights = jnp.where(near, jnp.exp(masked - peak), 0.0)
        scale = jnp.exp(before - peak)
        row_max[...] = peak
        row_total[...] = row_total[...] * scale + jnp.sum(weights, axis=1, keepdims=True)
        acc[...] = acc[...] * scale + jnp.dot(
            weights.astype(jnp.bfloat16), values, preferred_element_type=jnp.float32
        )

    def meet(zz, yy, half):
        def one(p, carry):
            arrived(zz, yy, 1 - core, half * group + p)
            return carry
        lax.fori_loop(0, group, one, 0)
        compute(zz, yy, half)

    def visited(distance, side, reach, origin):
        place = origin + jnp.where(side == 0, -distance, distance)
        inside = (distance >= 0) & (distance < reach) & (place >= 0) & (place < reach)
        return place, inside & jnp.logical_or(distance > 0, side == 0)

    def other_columns(body):
        if grid_fast == 2:
            body(1 - y)
            return
        def one(i, carry):
            yy, valid = visited(i // 2 + 1, lax.rem(i, 2), grid_fast, y)
            @pl.when(valid)
            def _():
                body(yy)
            return carry
        lax.fori_loop(0, 2 * (grid_fast - 1), one, 0)

    def along(zz, piece, side, act):
        each((2, 3, 0, 1, 4), (yes, yes, side == 1, side == 0, yes), zz, y, piece, False, act)

    def across(zz, yy, piece, act):
        each((2, 3, 4), (yy > y, yy < y, yes), zz, yy, piece, False, act)

    def receive(zz, yy, piece):
        arrived(zz, yy, core, piece)
        across(zz, yy, piece, start)

    farthest = jnp.where(2 * z >= grid_slow, 0, grid_slow - 1)

    def event(e, carry):
        distance = e // (2 * PIECES)
        piece = lax.rem(e // 2, PIECES)
        side = lax.rem(e, 2)
        half = piece // group

        @pl.when(e == 2 * PIECES * grid_slow)
        def _():
            for p in range(PIECES):
                each((2, 3, 0, 1, 4), (yes,) * 5, z, y, p, True, finish)

        zz, valid = visited(distance, side, grid_slow, z)
        @pl.when(valid & (distance > 0))
        def _():
            arrived(zz, y, core, piece)
            along(zz, piece, side, start)

        z1, valid1 = visited(distance - 1, side, grid_slow, z)
        z2, valid2 = visited(distance - 2, side, grid_slow, z)
        @pl.when(valid2)
        def _():
            other_columns(lambda yy: receive(z2, yy, piece))
            @pl.when(distance > 2)
            def _():
                along(z2, piece, side, finish)

        z3, valid3 = visited(distance - 3, side, grid_slow, z)
        @pl.when(valid3)
        def _():
            other_columns(lambda yy: across(z3, yy, piece, finish))

        near = valid1 & (lax.rem(piece, group) == 0)
        if grid_fast == 2:
            far = valid2 & (lax.rem(piece, group) == group - 1) & (z2 != farthest)
            @pl.when(near | far)
            def _():
                def one(i, carry):
                    @pl.when(jnp.where(i == 0, near, far))
                    def _():
                        meet(jnp.where(i == 0, z1, z2), jnp.where(i == 0, y, 1 - y), half)
                    return carry
                lax.fori_loop(0, 2, one, 0)
        else:
            @pl.when(near)
            def _():
                meet(z1, y, half)
            @pl.when(valid2 & (lax.rem(piece, group) == group - 1))
            def _():
                other_columns(lambda yy: meet(z2, yy, half))
        return carry

    lax.fori_loop(0, 2 * PIECES * (grid_slow + 2), event, 0)
    if grid_fast == 2:
        def last_pair(i, carry):
            cc = jnp.where(i == 0, core, 1 - core)
            @pl.when(i == 1)
            def _():
                for p in range(PIECES):
                    arrived(farthest, 1 - y, 1 - core, p)
            compute_core(farthest, 1 - y, cc)
            return carry
        lax.fori_loop(0, CORES, last_pair, 0)

    total = row_total[...]
    density = row_max[...] + jnp.log(total)
    dens_ref[...] = jnp.transpose(jnp.broadcast_to(density, (rows, rows)))[:1, :]
    mean_ref[...] = (acc[...] / total).astype(mean_ref.dtype)

    for e in range(2 * PIECES):
        last, valid = visited(grid_slow - 1, e % 2, grid_slow, z)
        @pl.when(valid)
        def _():
            other_columns(lambda yy: across(last, yy, e // 2, finish))


def per_device(device_count, embeddings, labels, row_slot):
    rows, width = embeddings.shape
    grid_slow, grid_fast = chip_grid(device_count)
    chips = device_count // CORES
    vmem = pl.BlockSpec(memory_space=pltpu.VMEM)
    density, mean = pl.pallas_call(
        functools.partial(kernel, grid_slow, grid_fast),
        out_shape=(
            pltpu.VMEM((1, rows), jnp.float32),
            pltpu.VMEM((rows, width), jnp.bfloat16),
        ),
        in_specs=[pl.BlockSpec(memory_space=pl.ANY), pl.BlockSpec(memory_space=pl.ANY)],
        out_specs=(vmem, vmem),
        scratch_shapes=[
            pltpu.VMEM((device_count * rows, width), jnp.bfloat16),
            pltpu.VMEM((device_count, 1, rows), jnp.int32),
            pltpu.VMEM((rows, width), jnp.bfloat16),
            pltpu.VMEM((rows, width), jnp.float32),
            pltpu.VMEM((rows, 1), jnp.float32),
            pltpu.VMEM((rows, 1), jnp.float32),
            pltpu.SemaphoreType.DMA((5, chips * PIECES)),
            pltpu.SemaphoreType.DMA((device_count * PIECES,)),
            pltpu.SemaphoreType.DMA((5, chips)),
            pltpu.SemaphoreType.DMA((device_count,)),
            pltpu.SemaphoreType.DMA((PIECES + 1,)),
            pltpu.SemaphoreType.DMA((1,)),
        ],
        compiler_params=pltpu.CompilerParams(collective_id=0, has_side_effects=True),
    )(embeddings, labels.reshape(1, rows))
    return density.reshape(rows), mean


def solution(mesh):
    return jax.shard_map(
        functools.partial(per_device, mesh.shape["docs"]),
        mesh=mesh,
        in_specs=(P(("groups", "docs"), None), P(("groups", "docs")), P(("groups", "docs"))),
        out_specs=(P(("groups", "docs")), P(("groups", "docs"), None)),
        check_vma=False,
    )
```
